32 devices in a mesh: users: 16 (over z, x, core), ctx: 2 (over y).
Axes of the slice: x: 2, y: 2, z: 4, core: 2. Of those that a mesh axis runs over, the one named last changes fastest.
Arguments:
- event_embed: bfloat16 [512, 16, 2048], P(('users', 'ctx')), may hold values from -6 to 6
- event_time_bucket: int32 [16, 2048], P('users', 'ctx'), may hold values from 0 to 127
- time_table: float32 [128, 512], replicated, may hold values from -6 to 6
- history_length: int32 [16], P('users'), may hold values from 512 to 2048, as said below
- w_proj: bfloat16 [512, 2048], replicated, may hold values from -0.25 to 0.25
- w_out: bfloat16 [512, 512], replicated, may hold values from -0.25 to 0.25
Outputs:
- layer_out: bfloat16 [16, 2048, 512], P('users', 'ctx')
The draws below stay inside these ranges and needn't reach their ends.
Inputs may be any that keep to these rules, and one draw needn't show every extreme that they name: `history_length`: one user in every draw has a full history of 2048 events.
All inputs are finite; a program needn't handle non-finite values.
Results may differ from the reference program's by a relative error of at most 0.0068.
Values may be sent and summed in bfloat16 or wider, within the bound.
A program may use at most 64 MiB of HBM per device.

```python
import jax
import jax.numpy as jnp
from jax import lax

D = 512
H = 8
HEAD_DIM = 64
BUCKETS = 128
BAND = 512
PREFIX = 512
EV_DEV = 1024
USERS = 16
EVENTS = 2048


def draw_history_length(key, part):
    rough = jax.random.randint(key, (USERS,), EVENTS // 4, EVENTS + 1)
    chosen = jax.random.randint(jax.random.fold_in(key, 7), (), 0, USERS)
    return jnp.where(jnp.arange(USERS) == chosen, EVENTS, rough).astype(jnp.int32)


def plant(array, stream_key, low, top_value):
    dims = array.shape
    index_at = [jax.random.randint(jax.random.fold_in(stream_key, axis), (), 0, dims[axis]) for axis in range(len(dims))]
    array = array.at[tuple(index_at)].set(low)
    longest = dims.index(max(dims))
    index_at[longest] = (index_at[longest] + 1) % dims[longest]
    return array.at[tuple(index_at)].set(top_value)


def block_levels(own_key, extent, pieces, smallest, largest):
    def one(axis_at, shards_of):
        draws = jax.random.uniform(jax.random.fold_in(jax.random.fold_in(own_key, 6), axis_at), (shards_of,), jnp.float32, smallest / len(pieces), largest / len(pieces))
        return jnp.repeat(jnp.exp(draws), extent[axis_at] // shards_of).reshape((-1,) + (1,) * (len(extent) - axis_at - 1))

    gain = one(*pieces[0])
    for cut in pieces[1:]:
        gain = gain * one(*cut)
    return gain


def bell_draw(key, extent, scale, reach, split=(), kind=jnp.bfloat16):
    level = block_levels(key, extent, split, -0.22, 0.18) if split else 1.0
    values = jax.random.normal(key, extent, jnp.float32) * scale * level
    return jnp.minimum(jnp.maximum(values, -reach), reach).astype(kind)


def setup_inputs(seed: int = 0) -> dict:
    splits = jax.random.split(jax.random.key(seed), 7)
    return {
        "event_embed": bell_draw(splits[0], (D, USERS, EVENTS), 1.0, 6.0, ((0, 32),)),
        "event_time_bucket": plant(jax.random.randint(splits[1], (USERS, EVENTS), 0, BUCKETS), jax.random.fold_in(splits[1], 1), 0, BUCKETS - 1).astype(jnp.int32),
        "time_table": bell_draw(splits[2], (BUCKETS, D), 1.0, 6.0, (), jnp.float32),
        "history_length": draw_history_length(jax.random.fold_in(splits[6], 71), 0),
        "w_proj": bell_draw(splits[4], (D, 4 * D), D ** -0.5, 0.25),
        "w_out": bell_draw(splits[5], (D, D), D ** -0.5, 0.25),
    }


def one_user(embed_cols, bucket_row, length_one, time_table, w_proj, w_out):
    events = embed_cols.T.astype(jnp.float32) + time_table[bucket_row]
    mean_square = lax.optimization_barrier(lax.optimization_barrier(jnp.mean(events * events, axis=1, keepdims=True)))
    normed = (events * lax.rsqrt(mean_square + 1e-05)).astype(jnp.bfloat16)
    projected = jax.nn.silu(jnp.dot(normed, w_proj, preferred_element_type=jnp.float32)).astype(jnp.bfloat16)
    gating = projected[:, :D]
    value_rows = projected[:, D:2 * D]
    query_rows = projected[:, 2 * D:3 * D]
    key_row_matrix = projected[:, 3 * D:]
    pad_keys = jnp.concatenate([jnp.zeros((BAND, D), jnp.bfloat16), key_row_matrix], axis=0)
    pad_values = jnp.concatenate([jnp.zeros((BAND, D), jnp.bfloat16), value_rows], axis=0)
    q_block = min(512, EV_DEV)
    prefix_keys = key_row_matrix[:PREFIX].astype(jnp.float32).reshape(PREFIX, H, HEAD_DIM)
    prefix_value_rows = value_rows[:PREFIX].astype(jnp.float32).reshape(PREFIX, H, HEAD_DIM)
    prefix_position = jnp.arange(PREFIX, dtype=jnp.int32)
    outputs = []
    for position_shift in range(0, EVENTS, q_block):
        query_pos = position_shift + jnp.arange(q_block, dtype=jnp.int32)
        window_pos = position_shift - BAND + jnp.arange(BAND + q_block, dtype=jnp.int32)
        live_query = query_pos < length_one
        window_ok = (window_pos[None, :] >= 0) & (window_pos[None, :] < length_one) & (window_pos[None, :] <= query_pos[:, None])
        window_ok = window_ok & ((window_pos[None, :] > query_pos[:, None] - BAND) | (window_pos[None, :] < PREFIX)) & live_query[:, None]
        prefix_ok = (prefix_position[None, :] < position_shift - BAND) & (prefix_position[None, :] < length_one) & (prefix_position[None, :] <= query_pos[:, None]) & live_query[:, None]
        key_count = lax.optimization_barrier(jnp.sum(window_ok.astype(jnp.int32), axis=1)) + lax.optimization_barrier(jnp.sum(prefix_ok.astype(jnp.int32), axis=1))
        divisor = jnp.maximum(key_count, 1).astype(jnp.float32)
        query_block = query_rows[position_shift:position_shift + q_block].astype(jnp.float32).reshape(q_block, H, HEAD_DIM)
        window_keys = pad_keys[position_shift:position_shift + BAND + q_block].astype(jnp.float32).reshape(-1, H, HEAD_DIM)
        window_values = pad_values[position_shift:position_shift + BAND + q_block].astype(jnp.float32).reshape(-1, H, HEAD_DIM)
        window_scores = jnp.einsum('qhe,khe->hqk', query_block, window_keys)
        prefix_scores = jnp.einsum('qhe,khe->hqk', query_block, prefix_keys)
        window_weights = (jnp.where(window_ok[None], jax.nn.silu(window_scores), 0.0) / divisor[None, :, None]).astype(jnp.bfloat16)
        prefix_weights = (jnp.where(prefix_ok[None], jax.nn.silu(prefix_scores), 0.0) / divisor[None, :, None]).astype(jnp.bfloat16)
        attended = jnp.einsum('hqk,khe->qhe', window_weights.astype(jnp.float32), window_values)
        attended = attended + jnp.einsum('hqk,khe->qhe', prefix_weights.astype(jnp.float32), prefix_value_rows)
        gated = (attended.reshape(q_block, D) * gating[position_shift:position_shift + q_block].astype(jnp.float32)).astype(jnp.bfloat16)
        outputs.append(jnp.dot(gated, w_out, preferred_element_type=jnp.float32).astype(jnp.bfloat16))
    return jnp.concatenate(outputs, axis=0)

def reference(event_embed, event_time_bucket, time_table, history_length, w_proj, w_out):
    user_ids = jnp.arange(USERS, dtype=jnp.int32)

    def per_user(user_id):
        embed_cols = lax.dynamic_index_in_dim(event_embed, user_id, 1, keepdims=False)
        bucket_row = lax.dynamic_index_in_dim(event_time_bucket, user_id, 0, keepdims=False)
        length_one = lax.dynamic_index_in_dim(history_length, user_id, 0, keepdims=False)
        return one_user(embed_cols, bucket_row, length_one, time_table, w_proj, w_out)
    return lax.map(per_user, user_ids)
```

```python
import functools

import jax
import jax.numpy as jnp
from jax import lax
from jax.experimental import pallas as pl
from jax.experimental.pallas import tpu as pltpu
from jax.sharding import PartitionSpec as P

H = 8
BAND = 512
PREFIX = 512
TILE = 256
MESH = pl.DeviceIdType.MESH
F32 = jnp.float32
BF16 = jnp.bfloat16


def exchange_kernel(users, local_len, src, bucket, recv, bucket_out, own_sems, send_sems, recv_sems, relay_send, relay_recv, bucket_sems):
    u = lax.axis_index("users")
    c = lax.axis_index("ctx")
    other = 1 - c

    barrier = pltpu.get_barrier_semaphore()

    def greet(k, carry):
        pl.semaphore_signal(barrier, inc=1, device_id=(lax.rem(u + k, users), c), device_id_type=MESH)
        return carry

    lax.fori_loop(1, users, greet, 0)
    pl.semaphore_signal(barrier, inc=1, device_id=(u, other), device_id_type=MESH)
    pl.semaphore_wait(barrier, users)

    def scatter(k):
        return pltpu.make_async_remote_copy(
            src_ref=src.at[lax.rem(u + k, users)],
            dst_ref=recv.at[u, c],
            send_sem=send_sems.at[k],
            recv_sem=recv_sems.at[k],
            device_id=(lax.rem(u + k, users), c),
            device_id_type=MESH,
        )

    def start_scatter(k, carry):
        scatter(k).start()
        return carry

    lax.fori_loop(1, users, start_scatter, 0)

    def relay(slot_ref, dst, k):
        return pltpu.make_async_remote_copy(
            src_ref=slot_ref,
            dst_ref=dst,
            send_sem=relay_send.at[k],
            recv_sem=relay_recv.at[k],
            device_id=(u, other),
            device_id_type=MESH,
        )

    def full(s, k):
        return relay(recv.at[s, c], recv.at[s, c], k)

    def part(s, k):
        return relay(recv.at[s, c, :, pl.ds(0, local_len)], recv.at[s, c, :, pl.ds(0, local_len)], k)

    keep = pltpu.make_async_copy(src.at[u], recv.at[u, c], own_sems.at[0])
    keep.start()
    bucket_keep = pltpu.make_async_copy(bucket, bucket_out.at[c], own_sems.at[1])
    bucket_keep.start()
    bucket_send = pltpu.make_async_remote_copy(
        src_ref=bucket,
        dst_ref=bucket_out.at[c],
        send_sem=bucket_sems.at[0],
        recv_sem=bucket_sems.at[1],
        device_id=(u, other),
        device_id_type=MESH,
    )
    bucket_send.start()

    def own_full():
        return relay(src.at[u], recv.at[u, c], 0)

    def own_part():
        return relay(src.at[u, :, pl.ds(0, local_len)], recv.at[u, c, :, pl.ds(0, local_len)], 0)

    pl.when(c == 0)(lambda: own_full().start())
    pl.when(c != 0)(lambda: own_part().start())

    def forward(k, carry):
        s = lax.rem(u + users - k, users)
        scatter(k).wait_recv()
        pl.when(c == 0)(lambda: full(s, k).start())
        pl.when(c != 0)(lambda: part(s, k).start())
        return carry

    lax.fori_loop(1, users, forward, 0)

    def finish(k, carry):
        scatter(k).wait_send()

        @pl.when(c == 0)
        def _():
            full(0, k).wait_send()
            part(0, k).wait_recv()

        @pl.when(c != 0)
        def _():
            part(0, k).wait_send()
            full(0, k).wait_recv()

        return carry

    lax.fori_loop(1, users, finish, 0)

    @pl.when(c == 0)
    def _():
        own_full().wait_send()
        own_part().wait_recv()

    @pl.when(c != 0)
    def _():
        own_part().wait_send()
        own_full().wait_recv()

    bucket_send.wait()
    bucket_keep.wait()
    keep.wait()


def exchange(by_user, bucket):
    users, width, events = by_user.shape
    local_len = bucket.shape[-1]
    return pl.pallas_call(
        functools.partial(exchange_kernel, users, local_len),
        out_shape=(
            jax.ShapeDtypeStruct((users, 2, width, events), BF16),
            jax.ShapeDtypeStruct((2, 1, local_len), jnp.int32),
        ),
        in_specs=[pl.BlockSpec(memory_space=pl.ANY)] * 2,
        out_specs=(pl.BlockSpec(memory_space=pl.ANY),) * 2,
        scratch_shapes=[
            pltpu.SemaphoreType.DMA((2,)),
            pltpu.SemaphoreType.DMA((users,)),
            pltpu.SemaphoreType.DMA((users,)),
            pltpu.SemaphoreType.DMA((users,)),
            pltpu.SemaphoreType.DMA((users,)),
            pltpu.SemaphoreType.DMA((2,)),
        ],
        compiler_params=pltpu.CompilerParams(collective_id=0, has_side_effects=True),
        name="exchange",
    )(by_user, bucket)


def silu(v):
    half = v * 0.5
    return half + half * jnp.tanh(half)


def gain(u):
    return u + u * jnp.tanh(u)


def dot(a, b):
    return jnp.dot(a, b, preferred_element_type=F32)


def dot_t(a, b):
    return lax.dot_general(a, b, (((1,), (1,)), ((), ())), preferred_element_type=F32)


def layer_kernel(wide, cols, bucket, table, length, w_proj, w_out, out, tab, keys, vals, queries, gates, gated):
    c = lax.axis_index("ctx")
    width = cols.shape[0]
    blocks = cols.shape[1] // TILE
    local_len = out.shape[0]
    strips = local_len // TILE
    own = (PREFIX + BAND) // TILE if wide else c * strips
    buckets = table.shape[0]
    head = width // H
    pair = 2 * head

    flipped = table[...].T
    upper = flipped.astype(BF16)
    tab[:, :buckets] = upper
    tab[:, buckets:] = (flipped - upper.astype(F32)).astype(BF16)

    def rows_of(b):
        ids = bucket[b]
        hot = (lax.broadcasted_iota(jnp.int32, (buckets, TILE), 0) == ids).astype(F32).astype(BF16)
        span = pl.ds(pl.multiple_of(b * TILE, TILE), TILE)
        events = cols[:, span].astype(F32) + dot(tab[...], jnp.concatenate([hot, hot], axis=0))
        mean_square = jnp.sum(events * events, axis=0, keepdims=True) * (1.0 / width)
        return (events * lax.rsqrt(mean_square + 1e-05)).astype(BF16).T

    def project_block(b):
        span = pl.ds(pl.multiple_of(b * TILE, TILE), TILE)
        normed = rows_of(b)
        vals[span, :] = silu(dot(normed, w_proj[:, width : 2 * width])).astype(BF16)
        keys[span, :] = silu(dot(normed, w_proj[:, 3 * width :])).astype(BF16)
        mine = (b >= own) & (b < own + strips)

        @pl.when(mine)
        def _():
            row = pl.ds(pl.multiple_of((b - own) * TILE, TILE), TILE)
            gates[row, :] = silu(dot(normed, w_proj[:, :width])).astype(BF16)
            queries[row, :] = silu(dot(normed, w_proj[:, 2 * width : 3 * width])).astype(BF16) * 0.5

    first = jnp.where(c == 0, own, 0)
    last = jnp.where(c == 0, own + strips, blocks)

    def project_step(b, carry):
        project_block(b)
        return carry

    lax.fori_loop(first, last, project_step, 0)

    lane = lax.broadcasted_iota(jnp.int32, (1, pair), 1)
    row_id = lax.broadcasted_iota(jnp.int32, (TILE, TILE), 0)
    col_id = lax.broadcasted_iota(jnp.int32, (TILE, TILE), 1)
    lower = row_id >= col_id

    def halves(rows):
        zero = jnp.zeros_like(rows)
        return jnp.where(lane < head, rows, zero), jnp.where(lane < head, zero, rows)

    def strip(s, carry):
        row = pl.ds(pl.multiple_of(s * TILE, TILE), TILE)
        position = c * local_len + s * TILE + lax.broadcasted_iota(jnp.int32, (TILE, 1), 0)
        count = jnp.minimum(position + 1, PREFIX + BAND).astype(F32)
        factor = jnp.where(position < length[0], 1.0 / count, 0.0)

        def put(p, attended):
            at = slice(p * pair, (p + 1) * pair)
            gated[:, at] = (attended * factor * gates[row, at].astype(F32)).astype(BF16)

        def at_block(ref, b, p, n=1):
            return ref[pl.ds(pl.multiple_of(b * TILE, TILE), n * TILE), p * pair : (p + 1) * pair]

        @pl.when(c == 0)
        def _():
            for p in range(H // 2):
                qs = halves(queries[row, p * pair : (p + 1) * pair])
                vs = halves(at_block(vals, own + s, p))
                k = at_block(keys, own + s, p)
                acc = jnp.zeros((TILE, pair), F32)
                for h in range(2):
                    w = jnp.where(lower, gain(dot_t(qs[h], k)), 0.0).astype(BF16)
                    acc = acc + dot(w, vs[h])

                def step(j, acc):
                    vs = halves(at_block(vals, own + j, p))
                    k = at_block(keys, own + j, p)
                    for h in range(2):
                        acc = acc + dot(gain(dot_t(qs[h], k)).astype(BF16), vs[h])
                    return acc

                put(p, lax.fori_loop(0, s, step, acc))

        @pl.when(c != 0)
        def _():
            for p in range(H // 2):
                qs = halves(queries[row, p * pair : (p + 1) * pair])
                k_pre = at_block(keys, 0, p, PREFIX // TILE)
                v_pre = halves(at_block(vals, 0, p, PREFIX // TILE))
                span = BAND // TILE
                k_win = at_block(keys, own + s - span, p, span + 1)
                v_win = halves(at_block(vals, own + s - span, p, span + 1))
                acc = jnp.zeros((TILE, pair), F32)
                for h in range(2):
                    acc = acc + dot(gain(dot_t(qs[h], k_pre)).astype(BF16), v_pre[h])
                    scores = dot_t(qs[h], k_win)
                    middle = gain(scores[:, TILE : span * TILE]).astype(BF16)
                    ends = gain(jnp.where(lower, scores[:, span * TILE :], scores[:, :TILE]))
                    oldest = jnp.where(lower, 0.0, ends).astype(BF16)
                    newest = jnp.where(lower, ends, 0.0).astype(BF16)
                    acc = acc + dot(jnp.concatenate([oldest, middle, newest], axis=1), v_win[h])
                put(p, acc)

        out[row, :] = dot(gated[...], w_out[...]).astype(BF16)
        return carry

    lax.fori_loop(0, strips, strip, 0)


def layer(wide, cols, bucket, table, length, w_proj, w_out, local_len):
    width, events = cols.shape
    vmem = pl.BlockSpec(memory_space=pltpu.VMEM)
    return pl.pallas_call(
        functools.partial(layer_kernel, wide),
        out_shape=jax.ShapeDtypeStruct((local_len, width), BF16),
        in_specs=[vmem, vmem, vmem, pl.BlockSpec(memory_space=pltpu.SMEM), vmem, vmem],
        out_specs=vmem,
        scratch_shapes=[
            pltpu.VMEM((width, 2 * table.shape[0]), BF16),
            pltpu.VMEM((events, width), BF16),
            pltpu.VMEM((events, width), BF16),
            pltpu.VMEM((local_len, width), BF16),
            pltpu.VMEM((local_len, width), BF16),
            pltpu.VMEM((TILE, width), BF16),
        ],
        name="layer",
    )(cols, bucket.reshape(-1, 1, TILE), table, length, w_proj, w_out)


def gather_wide(event_embed, bucket, ctx):
    local_len = bucket.shape[1]
    rows = lax.all_to_all(event_embed, "users", split_axis=1, concat_axis=0, tiled=True)[:, 0]
    users = lax.axis_size("users")
    all_buckets = lax.all_gather(bucket, "ctx", axis=1, tiled=True)
    start = lax.axis_index("ctx") * local_len

    def pieces(array, at):
        older = jnp.pad(array, ((0, 0), (BAND, 0)))
        band = lax.dynamic_slice_in_dim(older, at, BAND, 1)
        return jnp.concatenate([array[:, :PREFIX], band, lax.dynamic_slice_in_dim(array, at, local_len, 1)], axis=1)

    parts = jnp.stack([pieces(rows, at * local_len) for at in range(ctx)])
    got = lax.all_to_all(parts, "ctx", split_axis=0, concat_axis=0, tiled=True)
    width, span = got.shape[1] // users, got.shape[2]
    cols = got.reshape(ctx, users, width, span).transpose(1, 0, 2, 3).reshape(-1, span)
    return cols, pieces(all_buckets, start)


def local(event_embed, event_time_bucket, time_table, history_length, w_proj, w_out):
    ctx = lax.axis_size("ctx")
    local_len = event_time_bucket.shape[1]
    wide = ctx != 2 or ctx * local_len != PREFIX + BAND + local_len
    if wide:
        cols, bucket = gather_wide(event_embed, event_time_bucket, ctx)
    else:
        slots, bucket = exchange(event_embed.transpose(1, 0, 2), event_time_bucket)
        cols = slots.reshape(-1, slots.shape[-1])
    return layer(wide, cols, bucket, time_table, history_length, w_proj, w_out, local_len)[None]


def solution(mesh):
    return jax.shard_map(
        local,
        mesh=mesh,
        in_specs=(P(("users", "ctx"), None, None), P("users", "ctx"), P(), P("users"), P(), P()),
        out_specs=P("users", "ctx", None),
        check_vma=False,
    )
```

```python
import functools

import jax
import jax.numpy as jnp
from jax import lax
from jax.experimental import pallas as pl
from jax.experimental.pallas import tpu as pltpu
from jax.sharding import PartitionSpec as P

H = 8
BAND = 512
PREFIX = 512
TILE = 256
MESH = pl.DeviceIdType.MESH
F32 = jnp.float32
BF16 = jnp.bfloat16


def exchange_kernel(users, local_len, src, bucket, recv, bucket_out, own_sems, send_sems, recv_sems, relay_send, relay_recv, bucket_sems):
    u = lax.axis_index("users")
    c = lax.axis_index("ctx")
    other = 1 - c

    barrier = pltpu.get_barrier_semaphore()

    def greet(k, carry):
        pl.semaphore_signal(barrier, inc=1, device_id=(u ^ k, c), device_id_type=MESH)
        return carry

    lax.fori_loop(1, users, greet, 0)
    pl.semaphore_signal(barrier, inc=1, device_id=(u, other), device_id_type=MESH)
    pl.semaphore_wait(barrier, users)

    def scatter(k):
        return pltpu.make_async_remote_copy(
            src_ref=src.at[u ^ k],
            dst_ref=recv.at[u, c],
            send_sem=send_sems.at[k],
            recv_sem=recv_sems.at[k],
            device_id=(u ^ k, c),
            device_id_type=MESH,
        )

    def start_scatter(k, carry):
        scatter(k).start()
        return carry

    lax.fori_loop(1, users, start_scatter, 0)

    def relay(slot_ref, dst, k):
        return pltpu.make_async_remote_copy(
            src_ref=slot_ref,
            dst_ref=dst,
            send_sem=relay_send.at[k],
            recv_sem=relay_recv.at[k],
            device_id=(u, other),
            device_id_type=MESH,
        )

    def full(s, k):
        return relay(recv.at[s, c], recv.at[s, c], k)

    def part(s, k):
        return relay(recv.at[s, c, :, pl.ds(0, local_len)], recv.at[s, c, :, pl.ds(0, local_len)], k)

    keep = pltpu.make_async_copy(src.at[u], recv.at[u, c], own_sems.at[0])
    keep.start()
    bucket_keep = pltpu.make_async_copy(bucket, bucket_out.at[c], own_sems.at[1])
    bucket_keep.start()
    bucket_send = pltpu.make_async_remote_copy(
        src_ref=bucket,
        dst_ref=bucket_out.at[c],
        send_sem=bucket_sems.at[0],
        recv_sem=bucket_sems.at[1],
        device_id=(u, other),
        device_id_type=MESH,
    )
    bucket_send.start()

    def own_full():
        return relay(src.at[u], recv.at[u, c], 0)

    def own_part():
        return relay(src.at[u, :, pl.ds(0, local_len)], recv.at[u, c, :, pl.ds(0, local_len)], 0)

    pl.when(c == 0)(lambda: own_full().start())
    pl.when(c != 0)(lambda: own_part().start())

    def forward(k, carry):
        s = u ^ k
        scatter(k).wait_recv()
        pl.when(c == 0)(lambda: full(s, k).start())
        pl.when(c != 0)(lambda: part(s, k).start())
        return carry

    lax.fori_loop(1, users, forward, 0)

    def finish(k, carry):
        scatter(k).wait_send()

        @pl.when(c == 0)
        def _():
            full(0, k).wait_send()
            part(0, k).wait_recv()

        @pl.when(c != 0)
        def _():
            part(0, k).wait_send()
            full(0, k).wait_recv()

        return carry

    lax.fori_loop(1, users, finish, 0)

    @pl.when(c == 0)
    def _():
        own_full().wait_send()
        own_part().wait_recv()

    @pl.when(c != 0)
    def _():
        own_part().wait_send()
        own_full().wait_recv()

    bucket_send.wait()
    bucket_keep.wait()
    keep.wait()


def exchange(by_user, bucket):
    users, width, events = by_user.shape
    local_len = bucket.shape[-1]
    return pl.pallas_call(
        functools.partial(exchange_kernel, users, local_len),
        out_shape=(
            jax.ShapeDtypeStruct((users, 2, width, events), BF16),
            jax.ShapeDtypeStruct((2, 1, local_len), jnp.int32),
        ),
        in_specs=[pl.BlockSpec(memory_space=pl.ANY)] * 2,
        out_specs=(pl.BlockSpec(memory_space=pl.ANY),) * 2,
        scratch_shapes=[
            pltpu.SemaphoreType.DMA((2,)),
            pltpu.SemaphoreType.DMA((users,)),
            pltpu.SemaphoreType.DMA((users,)),
            pltpu.SemaphoreType.DMA((users,)),
            pltpu.SemaphoreType.DMA((users,)),
            pltpu.SemaphoreType.DMA((2,)),
        ],
        compiler_params=pltpu.CompilerParams(collective_id=0, has_side_effects=True),
        name="exchange",
    )(by_user, bucket)


def silu(v):
    half = v * 0.5
    return half + half * jnp.tanh(half)


def gain(u):
    return u + u * jnp.tanh(u)


def dot(a, b):
    return jnp.dot(a, b, preferred_element_type=F32)


def dot_t(a, b):
    return lax.dot_general(a, b, (((1,), (1,)), ((), ())), preferred_element_type=F32)


def layer_kernel(wide, cols, bucket, table, length, w_proj, w_out, out, tab, keys, vals, queries, gates, gated):
    c = lax.axis_index("ctx")
    width = cols.shape[0]
    blocks = cols.shape[1] // TILE
    local_len = out.shape[0]
    strips = local_len // TILE
    own = (PREFIX + BAND) // TILE if wide else c * strips
    buckets = table.shape[0]
    head = width // H
    pair = 2 * head

    flipped = table[...].T
    upper = flipped.astype(BF16)
    tab[:, :buckets] = upper
    tab[:, buckets:] = (flipped - upper.astype(F32)).astype(BF16)

    def rows_of(b):
        ids = bucket[b]
        hot = (lax.broadcasted_iota(jnp.int32, (buckets, TILE), 0) == ids).astype(F32).astype(BF16)
        span = pl.ds(pl.multiple_of(b * TILE, TILE), TILE)
        events = cols[:, span].astype(F32) + dot(tab[...], jnp.concatenate([hot, hot], axis=0))
        mean_square = jnp.sum(events * events, axis=0, keepdims=True) * (1.0 / width)
        return (events * lax.rsqrt(mean_square + 1e-05)).astype(BF16).T

    def project_block(b):
        span = pl.ds(pl.multiple_of(b * TILE, TILE), TILE)
        normed = rows_of(b)
        vals[span, :] = silu(dot(normed, w_proj[:, width : 2 * width])).astype(BF16)
        keys[span, :] = silu(dot(normed, w_proj[:, 3 * width :])).astype(BF16)
        mine = (b >= own) & (b < own + strips)

        @pl.when(mine)
        def _():
            row = pl.ds(pl.multiple_of((b - own) * TILE, TILE), TILE)
            gates[row, :] = silu(dot(normed, w_proj[:, :width])).astype(BF16)
            queries[row, :] = silu(dot(normed, w_proj[:, 2 * width : 3 * width])).astype(BF16) * 0.5

    first = jnp.where(c == 0, own, 0)
    last = jnp.where(c == 0, own + strips, blocks)

    def project_step(b, carry):
        project_block(b)
        return carry

    lax.fori_loop(first, last, project_step, 0)

    lane = lax.broadcasted_iota(jnp.int32, (1, pair), 1)
    row_id = lax.broadcasted_iota(jnp.int32, (TILE, TILE), 0)
    col_id = lax.broadcasted_iota(jnp.int32, (TILE, TILE), 1)
    lower = row_id >= col_id

    def halves(rows):
        zero = jnp.zeros_like(rows)
        return jnp.where(lane < head, rows, zero), jnp.where(lane < head, zero, rows)

    def strip(s, carry):
        row = pl.ds(pl.multiple_of(s * TILE, TILE), TILE)
        position = c * local_len + s * TILE + lax.broadcasted_iota(jnp.int32, (TILE, 1), 0)
        count = jnp.minimum(position + 1, PREFIX + BAND).astype(F32)
        factor = jnp.where(position < length[0], 1.0 / count, 0.0)

        def put(p, attended):
            at = slice(p * pair, (p + 1) * pair)
            gated[:, at] = (attended * factor * gates[row, at].astype(F32)).astype(BF16)

        def at_block(ref, b, p, n=1):
            return ref[pl.ds(pl.multiple_of(b * TILE, TILE), n * TILE), p * pair : (p + 1) * pair]

        @pl.when(c == 0)
        def _():
            for p in range(H // 2):
                qs = halves(queries[row, p * pair : (p + 1) * pair])
                vs = halves(at_block(vals, own + s, p))
                k = at_block(keys, own + s, p)
                acc = jnp.zeros((TILE, pair), F32)
                for h in range(2):
                    w = jnp.where(lower, gain(dot_t(qs[h], k)), 0.0).astype(BF16)
                    acc = acc + dot(w, vs[h])

                def step(j, acc):
                    vs = halves(at_block(vals, own + j, p))
                    k = at_block(keys, own + j, p)
                    for h in range(2):
                        acc = acc + dot(gain(dot_t(qs[h], k)).astype(BF16), vs[h])
                    return acc

                put(p, lax.fori_loop(0, s, step, acc))

        @pl.when(c != 0)
        def _():
            for p in range(H // 2):
                qs = halves(queries[row, p * pair : (p + 1) * pair])
                k_pre = at_block(keys, 0, p, PREFIX // TILE)
                v_pre = halves(at_block(vals, 0, p, PREFIX // TILE))
                span = BAND // TILE
                k_win = at_block(keys, own + s - span, p, span + 1)
                v_win = halves(at_block(vals, own + s - span, p, span + 1))
                acc = jnp.zeros((TILE, pair), F32)
                for h in range(2):
                    acc = acc + dot(gain(dot_t(qs[h], k_pre)).astype(BF16), v_pre[h])
                    scores = dot_t(qs[h], k_win)
                    middle = gain(scores[:, TILE : span * TILE]).astype(BF16)
                    ends = gain(jnp.where(lower, scores[:, span * TILE :], scores[:, :TILE]))
                    oldest = jnp.where(lower, 0.0, ends).astype(BF16)
                    newest = jnp.where(lower, ends, 0.0).astype(BF16)
                    acc = acc + dot(jnp.concatenate([oldest, middle, newest], axis=1), v_win[h])
                put(p, acc)

        out[row, :] = dot(gated[...], w_out[...]).astype(BF16)
        return carry

    lax.fori_loop(0, strips, strip, 0)


def layer(wide, cols, bucket, table, length, w_proj, w_out, local_len):
    width, events = cols.shape
    vmem = pl.BlockSpec(memory_space=pltpu.VMEM)
    return pl.pallas_call(
        functools.partial(layer_kernel, wide),
        out_shape=jax.ShapeDtypeStruct((local_len, width), BF16),
        in_specs=[vmem, vmem, vmem, pl.BlockSpec(memory_space=pltpu.SMEM), vmem, vmem],
        out_specs=vmem,
        scratch_shapes=[
            pltpu.VMEM((width, 2 * table.shape[0]), BF16),
            pltpu.VMEM((events, width), BF16),
            pltpu.VMEM((events, width), BF16),
            pltpu.VMEM((local_len, width), BF16),
            pltpu.VMEM((local_len, width), BF16),
            pltpu.VMEM((TILE, width), BF16),
        ],
        name="layer",
    )(cols, bucket.reshape(-1, 1, TILE), table, length, w_proj, w_out)


def gather_wide(event_embed, bucket, ctx):
    local_len = bucket.shape[1]
    rows = lax.all_to_all(event_embed, "users", split_axis=1, concat_axis=0, tiled=True)[:, 0]
    users = lax.axis_size("users")
    all_buckets = lax.all_gather(bucket, "ctx", axis=1, tiled=True)
    start = lax.axis_index("ctx") * local_len

    def pieces(array, at):
        older = jnp.pad(array, ((0, 0), (BAND, 0)))
        band = lax.dynamic_slice_in_dim(older, at, BAND, 1)
        return jnp.concatenate([array[:, :PREFIX], band, lax.dynamic_slice_in_dim(array, at, local_len, 1)], axis=1)

    parts = jnp.stack([pieces(rows, at * local_len) for at in range(ctx)])
    got = lax.all_to_all(parts, "ctx", split_axis=0, concat_axis=0, tiled=True)
    width, span = got.shape[1] // users, got.shape[2]
    cols = got.reshape(ctx, users, width, span).transpose(1, 0, 2, 3).reshape(-1, span)
    return cols, pieces(all_buckets, start)


def local(event_embed, event_time_bucket, time_table, history_length, w_proj, w_out):
    ctx = lax.axis_size("ctx")
    local_len = event_time_bucket.shape[1]
    users = lax.axis_size("users")
    wide = ctx != 2 or ctx * local_len != PREFIX + BAND + local_len or users & (users - 1) != 0
    if wide:
        cols, bucket = gather_wide(event_embed, event_time_bucket, ctx)
    else:
        slots, bucket = exchange(event_embed.transpose(1, 0, 2), event_time_bucket)
        cols = slots.reshape(-1, slots.shape[-1])
    return layer(wide, cols, bucket, time_table, history_length, w_proj, w_out, local_len)[None]


def solution(mesh):
    return jax.shard_map(
        local,
        mesh=mesh,
        in_specs=(P(("users", "ctx"), None, None), P("users", "ctx"), P(), P("users"), P(), P()),
        out_specs=P("users", "ctx", None),
        check_vma=False,
    )
```

```python
import functools

import jax
import jax.numpy as jnp
from jax import lax
from jax.experimental import pallas as pl
from jax.experimental.pallas import tpu as pltpu
from jax.sharding import PartitionSpec as P

H = 8
BAND = 512
PREFIX = 512
TILE = 256
MESH = pl.DeviceIdType.MESH
F32 = jnp.float32
BF16 = jnp.bfloat16


def silu(v):
    half = v * 0.5
    return half + half * jnp.tanh(half)


def gain(u):
    return u + u * jnp.tanh(u)


def dot(a, b):
    return jnp.dot(a, b, preferred_element_type=F32)


def dot_t(a, b):
    return lax.dot_general(a, b, (((1,), (1,)), ((), ())), preferred_element_type=F32)


def steps_of(c, own, strips, cols_at, bucket_at, table, length, w_proj, w_out, out, tab, keys, vals, queries, gates, gated):
    width = w_out.shape[0]
    local_len = out.shape[0]
    buckets = table.shape[0]
    head = width // H
    pair = 2 * head

    flipped = table[...].T
    upper = flipped.astype(BF16)
    tab[:, :buckets] = upper
    tab[:, buckets:] = (flipped - upper.astype(F32)).astype(BF16)

    def rows_of(b):
        ids = bucket_at(b)
        hot = (lax.broadcasted_iota(jnp.int32, (buckets, TILE), 0) == ids).astype(F32).astype(BF16)
        span = pl.ds(pl.multiple_of(b * TILE, TILE), TILE)
        events = cols_at(span).astype(F32) + dot(tab[...], jnp.concatenate([hot, hot], axis=0))
        mean_square = jnp.sum(events * events, axis=0, keepdims=True) * (1.0 / width)
        return (events * lax.rsqrt(mean_square + 1e-05)).astype(BF16).T

    def project_block(b):
        span = pl.ds(pl.multiple_of(b * TILE, TILE), TILE)
        normed = rows_of(b)
        vals[span, :] = silu(dot(normed, w_proj[:, width : 2 * width])).astype(BF16)
        keys[span, :] = silu(dot(normed, w_proj[:, 3 * width :])).astype(BF16)
        mine = (b >= own) & (b < own + strips)

        @pl.when(mine)
        def _():
            row = pl.ds(pl.multiple_of((b - own) * TILE, TILE), TILE)
            gates[row, :] = silu(dot(normed, w_proj[:, :width])).astype(BF16)
            queries[row, :] = silu(dot(normed, w_proj[:, 2 * width : 3 * width])).astype(BF16) * 0.5

    lane = lax.broadcasted_iota(jnp.int32, (1, pair), 1)
    row_id = lax.broadcasted_iota(jnp.int32, (TILE, TILE), 0)
    col_id = lax.broadcasted_iota(jnp.int32, (TILE, TILE), 1)
    lower = row_id >= col_id

    def halves(rows):
        zero = jnp.zeros_like(rows)
        return jnp.where(lane < head, rows, zero), jnp.where(lane < head, zero, rows)

    def strip(s, early):
        row = pl.ds(pl.multiple_of(s * TILE, TILE), TILE)
        position = c * local_len + s * TILE + lax.broadcasted_iota(jnp.int32, (TILE, 1), 0)
        count = jnp.minimum(position + 1, PREFIX + BAND).astype(F32)
        factor = jnp.where(position < length[0], 1.0 / count, 0.0)

        def put(p, attended):
            at = slice(p * pair, (p + 1) * pair)
            gated[:, at] = (attended * factor * gates[row, at].astype(F32)).astype(BF16)

        def at_block(ref, b, p, n=1):
            return ref[pl.ds(pl.multiple_of(b * TILE, TILE), n * TILE), p * pair : (p + 1) * pair]

        def early_pairs():
            for p in range(H // 2):
                qs = halves(queries[row, p * pair : (p + 1) * pair])
                vs = halves(at_block(vals, own + s, p))
                k = at_block(keys, own + s, p)
                acc = jnp.zeros((TILE, pair), F32)
                for h in range(2):
                    w = jnp.where(lower, gain(dot_t(qs[h], k)), 0.0).astype(BF16)
                    acc = acc + dot(w, vs[h])

                def step(j, acc):
                    vs = halves(at_block(vals, own + j, p))
                    k = at_block(keys, own + j, p)
                    for h in range(2):
                        acc = acc + dot(gain(dot_t(qs[h], k)).astype(BF16), vs[h])
                    return acc

                put(p, lax.fori_loop(0, s, step, acc))

        def later_pairs():
            for p in range(H // 2):
                qs = halves(queries[row, p * pair : (p + 1) * pair])
                k_pre = at_block(keys, 0, p, PREFIX // TILE)
                v_pre = halves(at_block(vals, 0, p, PREFIX // TILE))
                span = BAND // TILE
                k_win = at_block(keys, own + s - span, p, span + 1)
                v_win = halves(at_block(vals, own + s - span, p, span + 1))
                acc = jnp.zeros((TILE, pair), F32)
                for h in range(2):
                    acc = acc + dot(gain(dot_t(qs[h], k_pre)).astype(BF16), v_pre[h])
                    scores = dot_t(qs[h], k_win)
                    middle = gain(scores[:, TILE : span * TILE]).astype(BF16)
                    ends = gain(jnp.where(lower, scores[:, span * TILE :], scores[:, :TILE]))
                    oldest = jnp.where(lower, 0.0, ends).astype(BF16)
                    newest = jnp.where(lower, ends, 0.0).astype(BF16)
                    acc = acc + dot(jnp.concatenate([oldest, middle, newest], axis=1), v_win[h])
                put(p, acc)

        (early_pairs if early else later_pairs)()
        out[row, :] = dot(gated[...], w_out[...]).astype(BF16)

    return project_block, strip


def each(first, last, body):
    def step(i, carry):
        body(i)
        return carry

    lax.fori_loop(first, last, step, 0)


def layer_kernel(cols, bucket, table, length, w_proj, w_out, out, *scratch):
    c = lax.axis_index("ctx")
    blocks = cols.shape[1] // TILE
    strips = out.shape[0] // TILE
    own = (PREFIX + BAND) // TILE
    project_block, strip = steps_of(
        c, own, strips, lambda span: cols[:, span], lambda b: bucket[b], table, length, w_proj, w_out, out, *scratch
    )
    each(jnp.where(c == 0, own, 0), jnp.where(c == 0, own + strips, blocks), project_block)

    @pl.when(c == 0)
    def _():
        each(0, strips, lambda s: strip(s, True))

    @pl.when(c != 0)
    def _():
        each(0, strips, lambda s: strip(s, False))


def fused_kernel(
    users, src, bucket, table, length, w_proj, w_out, out,
    recv, ids, own_sems, send_sems, recv_sems, relay_send, relay_recv, bucket_sems, *scratch,
):
    u = lax.axis_index("users")
    c = lax.axis_index("ctx")
    other = 1 - c
    local_len = out.shape[0]
    half = local_len // 2
    strips = local_len // TILE

    def span_of(ch):
        if isinstance(ch, int) and ch == 0:
            return pl.ds(0, local_len)
        return pl.ds(pl.multiple_of(local_len + (ch - 1) * half, half), half)

    barrier = pltpu.get_barrier_semaphore()
    each(1, users, lambda k: pl.semaphore_signal(barrier, inc=1, device_id=(u ^ k, c), device_id_type=MESH))
    pl.semaphore_signal(barrier, inc=1, device_id=(u, other), device_id_type=MESH)
    pl.semaphore_wait(barrier, users)

    def scatter(ch, k):
        return pltpu.make_async_remote_copy(
            src_ref=src.at[u ^ k, :, span_of(ch)],
            dst_ref=recv.at[u, c, :, span_of(ch)],
            send_sem=send_sems.at[ch, k],
            recv_sem=recv_sems.at[ch, k],
            device_id=(u ^ k, c),
            device_id_type=MESH,
        )

    def relay(ch, k):
        return pltpu.make_async_remote_copy(
            src_ref=recv.at[u ^ k, c, :, span_of(ch)],
            dst_ref=recv.at[u ^ k, c, :, span_of(ch)],
            send_sem=relay_send.at[ch, k],
            recv_sem=relay_recv.at[ch, k],
            device_id=(u, other),
            device_id_type=MESH,
        )

    def incoming(ch, k):
        return pltpu.make_async_remote_copy(
            src_ref=recv.at[u ^ k, other, :, span_of(ch)],
            dst_ref=recv.at[u ^ k, other, :, span_of(ch)],
            send_sem=relay_send.at[ch, k],
            recv_sem=relay_recv.at[ch, k],
            device_id=(u, other),
            device_id_type=MESH,
        )

    keep = pltpu.make_async_copy(src.at[u], recv.at[u, c], own_sems.at[0])
    keep.start()
    id_keep = pltpu.make_async_copy(bucket, ids.at[c], own_sems.at[1])
    id_keep.start()
    id_send = pltpu.make_async_remote_copy(
        src_ref=bucket,
        dst_ref=ids.at[c],
        send_sem=bucket_sems.at[0],
        recv_sem=bucket_sems.at[1],
        device_id=(u, other),
        device_id_type=MESH,
    )
    id_send.start()
    for ch in range(3):
        each(1, users, lambda k: scatter(ch, k).start())
    keep.wait()
    relay(0, 0).start()

    def forward(ch):
        def one(k):
            scatter(ch, k).wait_recv()
            relay(ch, k).start()

        each(1, users, one)

    forward(0)
    id_keep.wait()
    id_send.wait()
    each(0, users, lambda k: incoming(0, k).wait_recv())

    def cols_at(span):
        return recv[:, :, :, span].reshape(w_out.shape[0], TILE)

    def ids_at(b):
        return ids[b // strips, :, pl.ds(pl.multiple_of(lax.rem(b, strips) * TILE, TILE), TILE)]

    project_block, strip = steps_of(
        c, c * strips, strips, cols_at, ids_at, table, length, w_proj, w_out, out, *scratch
    )
    part = strips // 2

    @pl.when(c == 0)
    def _():
        def phase(ph):
            each(ph * part, (ph + 1) * part, project_block)
            relay(ph + 1, 0).start()
            forward(ph + 1)
            each(ph * part, (ph + 1) * part, lambda s: strip(s, True))

        each(0, 2, phase)

        def sent(k):
            relay(1, k).wait_send()
            relay(2, k).wait_send()

        each(0, users, sent)

    @pl.when(c != 0)
    def _():
        each(0, strips, project_block)

        def phase(ph):
            each(1, users, lambda k: scatter(ph + 1, k).wait_recv())
            each(0, users, lambda k: incoming(ph + 1, k).wait_recv())
            each(strips + ph * part, strips + (ph + 1) * part, project_block)
            each(ph * part, (ph + 1) * part, lambda s: strip(s, False))

        each(0, 2, phase)

    each(0, users, lambda k: relay(0, k).wait_send())
    for ch in range(3):
        each(1, users, lambda k: scatter(ch, k).wait_send())


def fused(by_user, bucket, table, length, w_proj, w_out):
    users, cols, events = by_user.shape
    width = w_out.shape[0]
    local_len = bucket.shape[-1]
    vmem = pl.BlockSpec(memory_space=pltpu.VMEM)
    far = pl.BlockSpec(memory_space=pl.ANY)
    sems = pltpu.SemaphoreType.DMA((3, users))
    return pl.pallas_call(
        functools.partial(fused_kernel, users),
        out_shape=jax.ShapeDtypeStruct((local_len, width), BF16),
        in_specs=[far, far, vmem, pl.BlockSpec(memory_space=pltpu.SMEM), vmem, vmem],
        out_specs=vmem,
        scratch_shapes=[
            pltpu.VMEM((users, 2, cols, events), BF16),
            pltpu.VMEM((2, 1, local_len), jnp.int32),
            pltpu.SemaphoreType.DMA((2,)),
            sems,
            sems,
            sems,
            sems,
            pltpu.SemaphoreType.DMA((2,)),
            *layer_scratch(table, width, events, local_len),
        ],
        compiler_params=pltpu.CompilerParams(collective_id=0, has_side_effects=True),
        name="fused",
    )(by_user, bucket, table, length, w_proj, w_out)


def layer_scratch(table, width, events, local_len):
    return [
        pltpu.VMEM((width, 2 * table.shape[0]), BF16),
        pltpu.VMEM((events, width), BF16),
        pltpu.VMEM((events, width), BF16),
        pltpu.VMEM((local_len, width), BF16),
        pltpu.VMEM((local_len, width), BF16),
        pltpu.VMEM((TILE, width), BF16),
    ]


def layer(cols, bucket, table, length, w_proj, w_out, local_len):
    width, events = cols.shape
    vmem = pl.BlockSpec(memory_space=pltpu.VMEM)
    return pl.pallas_call(
        layer_kernel,
        out_shape=jax.ShapeDtypeStruct((local_len, width), BF16),
        in_specs=[vmem, vmem, vmem, pl.BlockSpec(memory_space=pltpu.SMEM), vmem, vmem],
        out_specs=vmem,
        scratch_shapes=layer_scratch(table, width, events, local_len),
        name="layer",
    )(cols, bucket.reshape(-1, 1, TILE), table, length, w_proj, w_out)


def gather_wide(event_embed, bucket, ctx):
    local_len = bucket.shape[1]
    rows = lax.all_to_all(event_embed, "users", split_axis=1, concat_axis=0, tiled=True)[:, 0]
    users = lax.axis_size("users")
    all_buckets = lax.all_gather(bucket, "ctx", axis=1, tiled=True)
    start = lax.axis_index("ctx") * local_len

    def pieces(array, at):
        older = jnp.pad(array, ((0, 0), (BAND, 0)))
        band = lax.dynamic_slice_in_dim(older, at, BAND, 1)
        return jnp.concatenate([array[:, :PREFIX], band, lax.dynamic_slice_in_dim(array, at, local_len, 1)], axis=1)

    parts = jnp.stack([pieces(rows, at * local_len) for at in range(ctx)])
    got = lax.all_to_all(parts, "ctx", split_axis=0, concat_axis=0, tiled=True)
    width, span = got.shape[1] // users, got.shape[2]
    cols = got.reshape(ctx, users, width, span).transpose(1, 0, 2, 3).reshape(-1, span)
    return cols, pieces(all_buckets, start)


def local(event_embed, event_time_bucket, time_table, history_length, w_proj, w_out):
    ctx = lax.axis_size("ctx")
    local_len = event_time_bucket.shape[1]
    users = lax.axis_size("users")
    wide = ctx != 2 or ctx * local_len != PREFIX + BAND + local_len or users & (users - 1) != 0
    if wide:
        cols, bucket = gather_wide(event_embed, event_time_bucket, ctx)
        done = layer(cols, bucket, time_table, history_length, w_proj, w_out, local_len)
    else:
        by_user = event_embed.transpose(1, 0, 2)
        done = fused(by_user, event_time_bucket, time_table, history_length, w_proj, w_out)
    return done[None]


def solution(mesh):
    return jax.shard_map(
        local,
        mesh=mesh,
        in_specs=(P(("users", "ctx"), None, None), P("users", "ctx"), P(), P("users"), P(), P()),
        out_specs=P("users", "ctx", None),
        check_vma=False,
    )
```

```python
import functools

import jax
import jax.numpy as jnp
from jax import lax
from jax.experimental import pallas as pl
from jax.experimental.pallas import tpu as pltpu
from jax.sharding import PartitionSpec as P

H = 8
BAND = 512
PREFIX = 512
TILE = 256
MESH = pl.DeviceIdType.MESH
F32 = jnp.float32
BF16 = jnp.bfloat16


def silu(v):
    half = v * 0.5
    return half + half * jnp.tanh(half)


def gain(u):
    return u + u * jnp.tanh(u)


def dot(a, b):
    return jnp.dot(a, b, preferred_element_type=F32)


def dot_t(a, b):
    return lax.dot_general(a, b, (((1,), (1,)), ((), ())), preferred_element_type=F32)


def steps_of(c, own, strips, cols_at, bucket_at, table, length, w_proj, w_out, out, tab, keys, vals, queries, gates, gated):
    width = w_out.shape[0]
    local_len = out.shape[0]
    buckets = table.shape[0]
    head = width // H
    pair = 2 * head

    flipped = table[...].T
    upper = flipped.astype(BF16)
    tab[:, :buckets] = upper
    tab[:, buckets:] = (flipped - upper.astype(F32)).astype(BF16)

    def rows_of(b):
        ids = bucket_at(b)
        hot = (lax.broadcasted_iota(jnp.int32, (buckets, TILE), 0) == ids).astype(F32).astype(BF16)
        span = pl.ds(pl.multiple_of(b * TILE, TILE), TILE)
        events = cols_at(span).astype(F32) + dot(tab[...], jnp.concatenate([hot, hot], axis=0))
        mean_square = jnp.sum(events * events, axis=0, keepdims=True) * (1.0 / width)
        return (events * lax.rsqrt(mean_square + 1e-05)).astype(BF16).T

    def project_block(b):
        span = pl.ds(pl.multiple_of(b * TILE, TILE), TILE)
        normed = rows_of(b)
        vals[span, :] = silu(dot(normed, w_proj[:, width : 2 * width])).astype(BF16)
        keys[span, :] = silu(dot(normed, w_proj[:, 3 * width :])).astype(BF16)
        mine = (b >= own) & (b < own + strips)

        @pl.when(mine)
        def _():
            row = pl.ds(pl.multiple_of((b - own) * TILE, TILE), TILE)
            gates[row, :] = silu(dot(normed, w_proj[:, :width])).astype(BF16)
            queries[row, :] = silu(dot(normed, w_proj[:, 2 * width : 3 * width])).astype(BF16) * 0.5

    lane = lax.broadcasted_iota(jnp.int32, (1, pair), 1)
    row_id = lax.broadcasted_iota(jnp.int32, (TILE, TILE), 0)
    col_id = lax.broadcasted_iota(jnp.int32, (TILE, TILE), 1)
    lower = row_id >= col_id

    def halves(rows):
        zero = jnp.zeros_like(rows)
        return jnp.where(lane < head, rows, zero), jnp.where(lane < head, zero, rows)

    def strip(s, early):
        row = pl.ds(pl.multiple_of(s * TILE, TILE), TILE)
        position = c * local_len + s * TILE + lax.broadcasted_iota(jnp.int32, (TILE, 1), 0)
        count = jnp.minimum(position + 1, PREFIX + BAND).astype(F32)
        factor = jnp.where(position < length[0], 1.0 / count, 0.0)

        def put(p, attended):
            at = slice(p * pair, (p + 1) * pair)
            gated[:, at] = (attended * factor * gates[row, at].astype(F32)).astype(BF16)

        def at_block(ref, b, p, n=1):
            return ref[pl.ds(pl.multiple_of(b * TILE, TILE), n * TILE), p * pair : (p + 1) * pair]

        def early_pairs():
            for p in range(H // 2):
                qs = halves(queries[row, p * pair : (p + 1) * pair])
                vs = halves(at_block(vals, own + s, p))
                k = at_block(keys, own + s, p)
                if s > 0:
                    k_old = at_block(keys, own, p, s)
                    v_old = halves(at_block(vals, own, p, s))
                acc = jnp.zeros((TILE, pair), F32)
                for h in range(2):
                    w = jnp.where(lower, gain(dot_t(qs[h], k)), 0.0).astype(BF16)
                    acc = acc + dot(w, vs[h])
                    if s > 0:
                        acc = acc + dot(gain(dot_t(qs[h], k_old)).astype(BF16), v_old[h])
                put(p, acc)

        def later_pairs():
            for p in range(H // 2):
                qs = halves(queries[row, p * pair : (p + 1) * pair])
                k_pre = at_block(keys, 0, p, PREFIX // TILE)
                v_pre = halves(at_block(vals, 0, p, PREFIX // TILE))
                span = BAND // TILE
                k_win = at_block(keys, own + s - span, p, span + 1)
                v_win = halves(at_block(vals, own + s - span, p, span + 1))
                acc = jnp.zeros((TILE, pair), F32)
                for h in range(2):
                    acc = acc + dot(gain(dot_t(qs[h], k_pre)).astype(BF16), v_pre[h])
                    scores = dot_t(qs[h], k_win)
                    middle = gain(scores[:, TILE : span * TILE]).astype(BF16)
                    ends = gain(jnp.where(lower, scores[:, span * TILE :], scores[:, :TILE]))
                    oldest = jnp.where(lower, 0.0, ends).astype(BF16)
                    newest = jnp.where(lower, ends, 0.0).astype(BF16)
                    acc = acc + dot(jnp.concatenate([oldest, middle, newest], axis=1), v_win[h])
                put(p, acc)

        (early_pairs if early else later_pairs)()
        out[row, :] = dot(gated[...], w_out[...]).astype(BF16)

    return project_block, strip


def each(first, last, body):
    def step(i, carry):
        body(i)
        return carry

    lax.fori_loop(first, last, step, 0)


def layer_kernel(cols, bucket, table, length, w_proj, w_out, out, *scratch):
    c = lax.axis_index("ctx")
    blocks = cols.shape[1] // TILE
    strips = out.shape[0] // TILE
    own = (PREFIX + BAND) // TILE
    project_block, strip = steps_of(
        c, own, strips, lambda span: cols[:, span], lambda b: bucket[b], table, length, w_proj, w_out, out, *scratch
    )
    each(jnp.where(c == 0, own, 0), jnp.where(c == 0, own + strips, blocks), project_block)

    @pl.when(c == 0)
    def _():
        for s in range(strips):
            strip(s, True)

    @pl.when(c != 0)
    def _():
        each(0, strips, lambda s: strip(s, False))


def fused_kernel(
    users, src, bucket, table, length, w_proj, w_out, out,
    recv, ids, own_sems, send_sems, recv_sems, relay_send, relay_recv, bucket_sems, *scratch,
):
    u = lax.axis_index("users")
    c = lax.axis_index("ctx")
    other = 1 - c
    local_len = out.shape[0]
    strips = local_len // TILE

    def span_of(ch):
        if isinstance(ch, int) and ch == 0:
            return pl.ds(0, local_len)
        return pl.ds(pl.multiple_of(local_len + (ch - 1) * TILE, TILE), TILE)

    barrier = pltpu.get_barrier_semaphore()
    each(1, users, lambda k: pl.semaphore_signal(barrier, inc=1, device_id=(u ^ k, c), device_id_type=MESH))
    pl.semaphore_signal(barrier, inc=1, device_id=(u, other), device_id_type=MESH)
    pl.semaphore_wait(barrier, users)

    def scatter(ch, k):
        return pltpu.make_async_remote_copy(
            src_ref=src.at[u ^ k, :, span_of(ch)],
            dst_ref=recv.at[u, c, :, span_of(ch)],
            send_sem=send_sems.at[ch, k],
            recv_sem=recv_sems.at[ch, k],
            device_id=(u ^ k, c),
            device_id_type=MESH,
        )

    def relay(ch, k):
        return pltpu.make_async_remote_copy(
            src_ref=recv.at[u ^ k, c, :, span_of(ch)],
            dst_ref=recv.at[u ^ k, c, :, span_of(ch)],
            send_sem=relay_send.at[ch, k],
            recv_sem=relay_recv.at[ch, k],
            device_id=(u, other),
            device_id_type=MESH,
        )

    def incoming(ch, k):
        return pltpu.make_async_remote_copy(
            src_ref=recv.at[u ^ k, other, :, span_of(ch)],
            dst_ref=recv.at[u ^ k, other, :, span_of(ch)],
            send_sem=relay_send.at[ch, k],
            recv_sem=relay_recv.at[ch, k],
            device_id=(u, other),
            device_id_type=MESH,
        )

    keep = pltpu.make_async_copy(src.at[u], recv.at[u, c], own_sems.at[0])
    keep.start()
    id_keep = pltpu.make_async_copy(bucket, ids.at[c], own_sems.at[1])
    id_keep.start()
    id_send = pltpu.make_async_remote_copy(
        src_ref=bucket,
        dst_ref=ids.at[c],
        send_sem=bucket_sems.at[0],
        recv_sem=bucket_sems.at[1],
        device_id=(u, other),
        device_id_type=MESH,
    )
    id_send.start()
    each(1, users, lambda k: scatter(0, k).start())
    each(1, strips + 1, lambda ch: each(1, users, lambda k: scatter(ch, k).start()))
    keep.wait()
    relay(0, 0).start()

    def forward(ch):
        def one(k):
            scatter(ch, k).wait_recv()
            relay(ch, k).start()

        each(1, users, one)

    forward(0)
    id_keep.wait()
    id_send.wait()
    each(0, users, lambda k: incoming(0, k).wait_recv())

    def cols_at(span):
        return recv[:, :, :, span].reshape(w_out.shape[0], TILE)

    def ids_at(b):
        return ids[b // strips, :, pl.ds(pl.multiple_of(lax.rem(b, strips) * TILE, TILE), TILE)]

    project_block, strip = steps_of(
        c, c * strips, strips, cols_at, ids_at, table, length, w_proj, w_out, out, *scratch
    )
    part = strips // 2

    @pl.when(c == 0)
    def _():
        def pass_on(ch):
            relay(ch, 0).start()
            forward(ch)

        each(0, part, project_block)
        pass_on(1)
        each(part, strips, project_block)
        for s in range(strips):
            if s + 2 <= strips:
                pass_on(s + 2)
            strip(s, True)
        each(1, strips + 1, lambda ch: each(0, users, lambda k: relay(ch, k).wait_send()))

    @pl.when(c != 0)
    def _():
        each(0, strips, project_block)

        def phase(ph):
            each(1, users, lambda k: scatter(ph + 1, k).wait_recv())
            each(0, users, lambda k: incoming(ph + 1, k).wait_recv())
            project_block(strips + ph)
            strip(ph, False)

        each(0, strips, phase)

    each(0, users, lambda k: relay(0, k).wait_send())
    each(1, users, lambda k: scatter(0, k).wait_send())
    each(1, strips + 1, lambda ch: each(1, users, lambda k: scatter(ch, k).wait_send()))


def fused(by_user, bucket, table, length, w_proj, w_out):
    users, cols, events = by_user.shape
    width = w_out.shape[0]
    local_len = bucket.shape[-1]
    vmem = pl.BlockSpec(memory_space=pltpu.VMEM)
    far = pl.BlockSpec(memory_space=pl.ANY)
    sems = pltpu.SemaphoreType.DMA((1 + local_len // TILE, users))
    return pl.pallas_call(
        functools.partial(fused_kernel, users),
        out_shape=jax.ShapeDtypeStruct((local_len, width), BF16),
        in_specs=[far, far, vmem, pl.BlockSpec(memory_space=pltpu.SMEM), vmem, vmem],
        out_specs=vmem,
        scratch_shapes=[
            pltpu.VMEM((users, 2, cols, events), BF16),
            pltpu.VMEM((2, 1, local_len), jnp.int32),
            pltpu.SemaphoreType.DMA((2,)),
            sems,
            sems,
            sems,
            sems,
            pltpu.SemaphoreType.DMA((2,)),
            *layer_scratch(table, width, events, local_len),
        ],
        compiler_params=pltpu.CompilerParams(collective_id=0, has_side_effects=True),
        name="fused",
    )(by_user, bucket, table, length, w_proj, w_out)


def layer_scratch(table, width, events, local_len):
    return [
        pltpu.VMEM((width, 2 * table.shape[0]), BF16),
        pltpu.VMEM((events, width), BF16),
        pltpu.VMEM((events, width), BF16),
        pltpu.VMEM((local_len, width), BF16),
        pltpu.VMEM((local_len, width), BF16),
        pltpu.VMEM((TILE, width), BF16),
    ]


def layer(cols, bucket, table, length, w_proj, w_out, local_len):
    width, events = cols.shape
    vmem = pl.BlockSpec(memory_space=pltpu.VMEM)
    return pl.pallas_call(
        layer_kernel,
        out_shape=jax.ShapeDtypeStruct((local_len, width), BF16),
        in_specs=[vmem, vmem, vmem, pl.BlockSpec(memory_space=pltpu.SMEM), vmem, vmem],
        out_specs=vmem,
        scratch_shapes=layer_scratch(table, width, events, local_len),
        name="layer",
    )(cols, bucket.reshape(-1, 1, TILE), table, length, w_proj, w_out)


def gather_wide(event_embed, bucket, ctx):
    local_len = bucket.shape[1]
    rows = lax.all_to_all(event_embed, "users", split_axis=1, concat_axis=0, tiled=True)[:, 0]
    users = lax.axis_size("users")
    all_buckets = lax.all_gather(bucket, "ctx", axis=1, tiled=True)
    start = lax.axis_index("ctx") * local_len

    def pieces(array, at):
        older = jnp.pad(array, ((0, 0), (BAND, 0)))
        band = lax.dynamic_slice_in_dim(older, at, BAND, 1)
        return jnp.concatenate([array[:, :PREFIX], band, lax.dynamic_slice_in_dim(array, at, local_len, 1)], axis=1)

    parts = jnp.stack([pieces(rows, at * local_len) for at in range(ctx)])
    got = lax.all_to_all(parts, "ctx", split_axis=0, concat_axis=0, tiled=True)
    width, span = got.shape[1] // users, got.shape[2]
    cols = got.reshape(ctx, users, width, span).transpose(1, 0, 2, 3).reshape(-1, span)
    return cols, pieces(all_buckets, start)


def local(event_embed, event_time_bucket, time_table, history_length, w_proj, w_out):
    ctx = lax.axis_size("ctx")
    local_len = event_time_bucket.shape[1]
    users = lax.axis_size("users")
    wide = ctx != 2 or ctx * local_len != PREFIX + BAND + local_len or users & (users - 1) != 0
    if wide:
        cols, bucket = gather_wide(event_embed, event_time_bucket, ctx)
        done = layer(cols, bucket, time_table, history_length, w_proj, w_out, local_len)
    else:
        by_user = event_embed.transpose(1, 0, 2)
        done = fused(by_user, event_time_bucket, time_table, history_length, w_proj, w_out)
    return done[None]


def solution(mesh):
    return jax.shard_map(
        local,
        mesh=mesh,
        in_specs=(P(("users", "ctx"), None, None), P("users", "ctx"), P(), P("users"), P(), P()),
        out_specs=P("users", "ctx", None),
        check_vma=False,
    )
```

```python
import functools

import jax
import jax.numpy as jnp
from jax import lax
from jax.experimental import pallas as pl
from jax.experimental.pallas import tpu as pltpu
from jax.sharding import PartitionSpec as P

H = 8
BAND = 512
PREFIX = 512
TILE = 256
MESH = pl.DeviceIdType.MESH
F32 = jnp.float32
BF16 = jnp.bfloat16


def silu(v):
    half = v * 0.5
    return half + half * jnp.tanh(half)


def gain(u):
    return u + u * jnp.tanh(u)


def dot(a, b):
    return jnp.dot(a, b, preferred_element_type=F32)


def dot_t(a, b):
    return lax.dot_general(a, b, (((1,), (1,)), ((), ())), preferred_element_type=F32)


def steps_of(c, own, strips, cols_at, bucket_at, table, length, w_proj, w_out, out, tab, keys, vals, queries, gates, gated):
    width = w_out.shape[0]
    local_len = out.shape[0]
    buckets = table.shape[0]
    head = width // H
    pair = 2 * head

    flipped = table[...].T
    upper = flipped.astype(BF16)
    tab[:, :buckets] = upper
    tab[:, buckets:] = (flipped - upper.astype(F32)).astype(BF16)

    def rows_of(b):
        ids = bucket_at(b)
        hot = (lax.broadcasted_iota(jnp.int32, (buckets, TILE), 0) == ids).astype(F32).astype(BF16)
        span = pl.ds(pl.multiple_of(b * TILE, TILE), TILE)
        events = cols_at(span).astype(F32) + dot(tab[...], jnp.concatenate([hot, hot], axis=0))
        mean_square = jnp.sum(events * events, axis=0, keepdims=True) * (1.0 / width)
        return (events * lax.rsqrt(mean_square + 1e-05)).astype(BF16).T

    def project_block(b):
        span = pl.ds(pl.multiple_of(b * TILE, TILE), TILE)
        normed = rows_of(b)
        vals[span, :] = silu(dot(normed, w_proj[:, width : 2 * width])).astype(BF16)
        keys[span, :] = silu(dot(normed, w_proj[:, 3 * width :])).astype(BF16)
        mine = (b >= own) & (b < own + strips)

        @pl.when(mine)
        def _():
            row = pl.ds(pl.multiple_of((b - own) * TILE, TILE), TILE)
            gates[row, :] = silu(dot(normed, w_proj[:, :width])).astype(BF16)
            queries[row, :] = silu(dot(normed, w_proj[:, 2 * width : 3 * width])).astype(BF16) * 0.5

    lane = lax.broadcasted_iota(jnp.int32, (1, pair), 1)
    row_id = lax.broadcasted_iota(jnp.int32, (TILE, TILE), 0)
    col_id = lax.broadcasted_iota(jnp.int32, (TILE, TILE), 1)
    lower = row_id >= col_id

    def halves(rows):
        zero = jnp.zeros_like(rows)
        return jnp.where(lane < head, rows, zero), jnp.where(lane < head, zero, rows)

    def strip(s, early):
        row = pl.ds(pl.multiple_of(s * TILE, TILE), TILE)
        position = c * local_len + s * TILE + lax.broadcasted_iota(jnp.int32, (TILE, 1), 0)
        count = jnp.minimum(position + 1, PREFIX + BAND).astype(F32)
        factor = jnp.where(position < length[0], 1.0 / count, 0.0)

        def put(p, attended):
            at = slice(p * pair, (p + 1) * pair)
            gated[:, at] = (attended * factor * gates[row, at].astype(F32)).astype(BF16)

        def at_block(ref, b, p, n=1):
            return ref[pl.ds(pl.multiple_of(b * TILE, TILE), n * TILE), p * pair : (p + 1) * pair]

        def early_pairs():
            for p in range(H // 2):
                qs = halves(queries[row, p * pair : (p + 1) * pair])
                vs = halves(at_block(vals, own + s, p))
                k = at_block(keys, own + s, p)
                if s > 0:
                    k_old = at_block(keys, own, p, s)
                    v_old = halves(at_block(vals, own, p, s))
                acc = jnp.zeros((TILE, pair), F32)
                for h in range(2):
                    w = jnp.where(lower, gain(dot_t(qs[h], k)), 0.0).astype(BF16)
                    acc = acc + dot(w, vs[h])
                    if s > 0:
                        acc = acc + dot(gain(dot_t(qs[h], k_old)).astype(BF16), v_old[h])
                put(p, acc)

        def later_pairs():
            for p in range(H // 2):
                qs = halves(queries[row, p * pair : (p + 1) * pair])
                k_pre = at_block(keys, 0, p, PREFIX // TILE)
                v_pre = halves(at_block(vals, 0, p, PREFIX // TILE))
                span = BAND // TILE
                k_win = at_block(keys, own + s - span, p, span + 1)
                v_win = halves(at_block(vals, own + s - span, p, span + 1))
                acc = jnp.zeros((TILE, pair), F32)
                for h in range(2):
                    acc = acc + dot(gain(dot_t(qs[h], k_pre)).astype(BF16), v_pre[h])
                    scores = dot_t(qs[h], k_win)
                    middle = gain(scores[:, TILE : span * TILE]).astype(BF16)
                    ends = gain(jnp.where(lower, scores[:, span * TILE :], scores[:, :TILE]))
                    oldest = jnp.where(lower, 0.0, ends).astype(BF16)
                    newest = jnp.where(lower, ends, 0.0).astype(BF16)
                    acc = acc + dot(jnp.concatenate([oldest, middle, newest], axis=1), v_win[h])
                put(p, acc)

        (early_pairs if early else later_pairs)()
        out[row, :] = dot(gated[...], w_out[...]).astype(BF16)

    return project_block, strip


def each(first, last, body):
    def step(i, carry):
        body(i)
        return carry

    lax.fori_loop(first, last, step, 0)


def layer_kernel(cols, bucket, table, length, w_proj, w_out, out, *scratch):
    c = lax.axis_index("ctx")
    blocks = cols.shape[1] // TILE
    strips = out.shape[0] // TILE
    own = (PREFIX + BAND) // TILE
    project_block, strip = steps_of(
        c, own, strips, lambda span: cols[:, span], lambda b: bucket[b], table, length, w_proj, w_out, out, *scratch
    )
    each(jnp.where(c == 0, own, 0), jnp.where(c == 0, own + strips, blocks), project_block)

    @pl.when(c == 0)
    def _():
        for s in range(strips):
            strip(s, True)

    @pl.when(c != 0)
    def _():
        each(0, strips, lambda s: strip(s, False))


def fused_kernel(
    users, src, bucket, table, length, w_proj, w_out, out,
    recv, ids, own_sems, send_sems, recv_sems, relay_send, relay_recv, bucket_sems, *scratch,
):
    u = lax.axis_index("users")
    c = lax.axis_index("ctx")
    other = 1 - c
    local_len = out.shape[0]
    strips = local_len // TILE

    def span_of(ch):
        if isinstance(ch, int) and ch == 0:
            return pl.ds(0, local_len)
        return pl.ds(pl.multiple_of(local_len + (ch - 1) * TILE, TILE), TILE)

    barrier = pltpu.get_barrier_semaphore()
    each(1, users, lambda k: pl.semaphore_signal(barrier, inc=1, device_id=(u ^ k, c), device_id_type=MESH))
    pl.semaphore_signal(barrier, inc=1, device_id=(u, other), device_id_type=MESH)
    pl.semaphore_wait(barrier, users)

    def scatter(ch, k):
        return pltpu.make_async_remote_copy(
            src_ref=src.at[u ^ k, :, span_of(ch)],
            dst_ref=recv.at[u, c, :, span_of(ch)],
            send_sem=send_sems.at[ch, k],
            recv_sem=recv_sems.at[ch, k],
            device_id=(u ^ k, c),
            device_id_type=MESH,
        )

    def relay(ch, k):
        return pltpu.make_async_remote_copy(
            src_ref=recv.at[u ^ k, c, :, span_of(ch)],
            dst_ref=recv.at[u ^ k, c, :, span_of(ch)],
            send_sem=relay_send.at[ch, k],
            recv_sem=relay_recv.at[ch, k],
            device_id=(u, other),
            device_id_type=MESH,
        )

    def incoming(ch, k):
        return pltpu.make_async_remote_copy(
            src_ref=recv.at[u ^ k, other, :, span_of(ch)],
            dst_ref=recv.at[u ^ k, other, :, span_of(ch)],
            send_sem=relay_send.at[ch, k],
            recv_sem=relay_recv.at[ch, k],
            device_id=(u, other),
            device_id_type=MESH,
        )

    keep = pltpu.make_async_copy(src.at[u], recv.at[u, c], own_sems.at[0])
    keep.start()
    id_keep = pltpu.make_async_copy(bucket, ids.at[c], own_sems.at[1])
    id_keep.start()
    id_send = pltpu.make_async_remote_copy(
        src_ref=bucket,
        dst_ref=ids.at[c],
        send_sem=bucket_sems.at[0],
        recv_sem=bucket_sems.at[1],
        device_id=(u, other),
        device_id_type=MESH,
    )
    id_send.start()
    each(1, users, lambda k: scatter(0, k).start())
    each(1, strips + 1, lambda ch: each(1, users, lambda k: scatter(ch, k).start()))
    keep.wait()
    relay(0, 0).start()

    def forward(ch):
        def one(k):
            scatter(ch, k).wait_recv()
            relay(ch, k).start()

        each(1, users, one)

    forward(0)
    def pass_on(ch):
        relay(ch, 0).start()
        forward(ch)

    @pl.when(c == 0)
    def _():
        pass_on(1)
        pass_on(2)

    id_keep.wait()
    id_send.wait()
    each(0, users, lambda k: incoming(0, k).wait_recv())

    def cols_at(span):
        return recv[:, :, :, span].reshape(w_out.shape[0], TILE)

    def ids_at(b):
        return ids[b // strips, :, pl.ds(pl.multiple_of(lax.rem(b, strips) * TILE, TILE), TILE)]

    project_block, strip = steps_of(
        c, c * strips, strips, cols_at, ids_at, table, length, w_proj, w_out, out, *scratch
    )
    part = strips // 2

    @pl.when(c == 0)
    def _():
        each(0, part, project_block)
        pass_on(3)
        each(part, strips, project_block)
        for s in range(strips):
            if s + 4 <= strips:
                pass_on(s + 4)
            strip(s, True)
        each(1, strips + 1, lambda ch: each(0, users, lambda k: relay(ch, k).wait_send()))

    @pl.when(c != 0)
    def _():
        each(0, strips, project_block)

        def phase(ph):
            each(1, users, lambda k: scatter(ph + 1, k).wait_recv())
            each(0, users, lambda k: incoming(ph + 1, k).wait_recv())
            project_block(strips + ph)
            strip(ph, False)

        each(0, strips, phase)

    each(0, users, lambda k: relay(0, k).wait_send())
    each(1, users, lambda k: scatter(0, k).wait_send())
    each(1, strips + 1, lambda ch: each(1, users, lambda k: scatter(ch, k).wait_send()))


def fused(by_user, bucket, table, length, w_proj, w_out):
    users, cols, events = by_user.shape
    width = w_out.shape[0]
    local_len = bucket.shape[-1]
    vmem = pl.BlockSpec(memory_space=pltpu.VMEM)
    far = pl.BlockSpec(memory_space=pl.ANY)
    sems = pltpu.SemaphoreType.DMA((1 + local_len // TILE, users))
    return pl.pallas_call(
        functools.partial(fused_kernel, users),
        out_shape=jax.ShapeDtypeStruct((local_len, width), BF16),
        in_specs=[far, far, vmem, pl.BlockSpec(memory_space=pltpu.SMEM), vmem, vmem],
        out_specs=vmem,
        scratch_shapes=[
            pltpu.VMEM((users, 2, cols, events), BF16),
            pltpu.VMEM((2, 1, local_len), jnp.int32),
            pltpu.SemaphoreType.DMA((2,)),
            sems,
            sems,
            sems,
            sems,
            pltpu.SemaphoreType.DMA((2,)),
            *layer_scratch(table, width, events, local_len),
        ],
        compiler_params=pltpu.CompilerParams(collective_id=0, has_side_effects=True),
        name="fused",
    )(by_user, bucket, table, length, w_proj, w_out)


def layer_scratch(table, width, events, local_len):
    return [
        pltpu.VMEM((width, 2 * table.shape[0]), BF16),
        pltpu.VMEM((events, width), BF16),
        pltpu.VMEM((events, width), BF16),
        pltpu.VMEM((local_len, width), BF16),
        pltpu.VMEM((local_len, width), BF16),
        pltpu.VMEM((TILE, width), BF16),
    ]


def layer(cols, bucket, table, length, w_proj, w_out, local_len):
    width, events = cols.shape
    vmem = pl.BlockSpec(memory_space=pltpu.VMEM)
    return pl.pallas_call(
        layer_kernel,
        out_shape=jax.ShapeDtypeStruct((local_len, width), BF16),
        in_specs=[vmem, vmem, vmem, pl.BlockSpec(memory_space=pltpu.SMEM), vmem, vmem],
        out_specs=vmem,
        scratch_shapes=layer_scratch(table, width, events, local_len),
        name="layer",
    )(cols, bucket.reshape(-1, 1, TILE), table, length, w_proj, w_out)


def gather_wide(event_embed, bucket, ctx):
    local_len = bucket.shape[1]
    rows = lax.all_to_all(event_embed, "users", split_axis=1, concat_axis=0, tiled=True)[:, 0]
    users = lax.axis_size("users")
    all_buckets = lax.all_gather(bucket, "ctx", axis=1, tiled=True)
    start = lax.axis_index("ctx") * local_len

    def pieces(array, at):
        older = jnp.pad(array, ((0, 0), (BAND, 0)))
        band = lax.dynamic_slice_in_dim(older, at, BAND, 1)
        return jnp.concatenate([array[:, :PREFIX], band, lax.dynamic_slice_in_dim(array, at, local_len, 1)], axis=1)

    parts = jnp.stack([pieces(rows, at * local_len) for at in range(ctx)])
    got = lax.all_to_all(parts, "ctx", split_axis=0, concat_axis=0, tiled=True)
    width, span = got.shape[1] // users, got.shape[2]
    cols = got.reshape(ctx, users, width, span).transpose(1, 0, 2, 3).reshape(-1, span)
    return cols, pieces(all_buckets, start)


def local(event_embed, event_time_bucket, time_table, history_length, w_proj, w_out):
    ctx = lax.axis_size("ctx")
    local_len = event_time_bucket.shape[1]
    users = lax.axis_size("users")
    wide = ctx != 2 or ctx * local_len != PREFIX + BAND + local_len or users & (users - 1) != 0
    if wide:
        cols, bucket = gather_wide(event_embed, event_time_bucket, ctx)
        done = layer(cols, bucket, time_table, history_length, w_proj, w_out, local_len)
    else:
        by_user = event_embed.transpose(1, 0, 2)
        done = fused(by_user, event_time_bucket, time_table, history_length, w_proj, w_out)
    return done[None]


def solution(mesh):
    return jax.shard_map(
        local,
        mesh=mesh,
        in_specs=(P(("users", "ctx"), None, None), P("users", "ctx"), P(), P("users"), P(), P()),
        out_specs=P("users", "ctx", None),
        check_vma=False,
    )
```
